32 devices in a mesh: space: 4 (over x, core), dir: 8 (over z, y).
Axes of the slice: x: 2, y: 2, z: 4, core: 2. Of those that a mesh axis runs over, the one named last changes fastest.
Arguments:
- phonon_heat_density: float32 [128, 40, 8, 4, 256], P('dir', None, 'space'), may hold values from 0.01 to 20, as said below
- directions: float32 [3, 128], replicated, may hold values from -1 to 1, as said below
- quad_weight: float32 [128], replicated, may hold values from 0 to 1, as said below
- mirror: int32 [3, 128], replicated, may hold values from 0 to 127, as said below
- band_courant: float32 [40], replicated, may hold values from 0.3 to 1.9
- relax_rate: float32 [40], replicated, may hold values from 0.05 to 0.95
- mode_heat_magnitude: float32 [40], replicated, may hold values from 0.5 to 2
- mode_pulsation: float32 [40], replicated, may hold values from 0.3 to 2.5
- wall_blocks: int32 [4, 16], P('space'), may hold values from 0 to 15, as said below
- wall_count: int32 [4], P('space'), may hold values from 0 to 16, as said below
- wall_facet: int32 [4, 16, 128], P('space'), may hold values from 0 to 6, as said below
Outputs:
- energy_out: float32 [128, 40, 8, 4, 256], P('dir', None, 'space')
- pseudo_kelvin_field: float32 [8, 4, 256], P('space')
The draws below stay inside these ranges and needn't reach their ends.
Inputs may be any that keep to these rules, and one draw needn't show every extreme that they name: Unit vectors with no zero component; negating any one component of a direction gives another of the directions. `quad_weight`: Positive, summing to 1, equal for directions that differ only in the signs of components. mirror[a, d] is the direction whose vector is that of d with component a negated. `phonon_heat_density`: Positive. `wall_blocks`: the entries of each row are distinct blocks of the tile; the first wall_count[t] of them are its wall blocks. `wall_count`: tiles t and t + 2 hold at most 16 wall blocks together; some pair holds exactly that, with one of its tiles at 16. `wall_facet`: 0 marks a cell that is no wall, and every cell of slots from wall_count[t] on; f from 1 to 6 names the facet normal along axis (f - 1) // 2, positive for odd f and negative for even f.
All inputs are finite; a program needn't handle non-finite values.
Results may differ from the reference program's by a relative error of at most 0.0003.
Values sent between devices are 32-bit elements; how exact they have to be, the bound alone decides.
A program may use at most 128 MiB of HBM per device.

```python
import math
import jax
import jax.numpy as jnp
from jax import lax

BANDS = 40
DIRS = 128
NBASE = 16
MESH_DEEP_COUNT = 256
LAYER_HIGH_COUNT = 4
STEPS = 2
NEWTON = 4
BLOCK = 128
WPAIR = 8
WMAX = 16
TILES = 4
MESH_WIDE_COUNT = 8
TILE_BLOCKS = 16


def direction_set(key):
    base_key = jax.random.fold_in(key, 101)
    first_key, second_key, third_key = jax.random.split(base_key, 3)
    cosine = jax.random.uniform(first_key, (NBASE,), jnp.float32, 0.15, 0.95)
    azimuth = jax.random.uniform(second_key, (NBASE,), jnp.float32, 0.15, 1.42)
    radial = jnp.sqrt(1.0 - cosine * cosine)
    base_vectors = jnp.stack([radial * jnp.cos(azimuth), radial * jnp.sin(azimuth), cosine])
    base_weight = jnp.exp(jax.random.uniform(third_key, (NBASE,), jnp.float32, jnp.log(0.3), jnp.log(3.0)))
    ordering = jax.random.permutation(jax.random.fold_in(key, 102), DIRS).astype(jnp.int32)
    octant = ordering // NBASE
    member = ordering % NBASE
    return (base_vectors, base_weight, ordering, octant, member)


def octant_bit(octant, axis_num):
    return octant // 2 ** axis_num % 2


def draw_directions(key, part):
    base_vectors, base_weight, ordering, octant, member = direction_set(key)
    rows = []
    for axis_num in range(3):
        signs = (1 - 2 * octant_bit(octant, axis_num)).astype(jnp.float32)
        rows.append(signs * base_vectors[axis_num][member])
    return jnp.stack(rows).astype(jnp.float32)


def draw_quad_weight(key, part):
    base_vectors, base_weight, ordering, octant, member = direction_set(key)
    return (base_weight[member] / (8.0 * jnp.sum(base_weight))).astype(jnp.float32)


def draw_mirror(key, part):
    base_vectors, base_weight, ordering, octant, member = direction_set(key)
    inverse = jnp.argsort(ordering).astype(jnp.int32)
    rows = []
    for axis_num in range(3):
        flipped = octant + (1 - 2 * octant_bit(octant, axis_num)) * 2 ** axis_num
        rows.append(inverse[flipped * NBASE + member])
    return jnp.stack(rows).astype(jnp.int32)


def draw_phonon_heat_density(key, part):
    cell_key, entry_key = jax.random.split(jax.random.fold_in(key, 1), 2)
    full_shape = (DIRS, BANDS, MESH_WIDE_COUNT, LAYER_HIGH_COUNT, MESH_DEEP_COUNT)
    scale = jnp.exp(jax.random.uniform(cell_key, (MESH_WIDE_COUNT, LAYER_HIGH_COUNT, MESH_DEEP_COUNT), jnp.float32, jnp.log(0.2), jnp.log(5.0)))
    factor = jnp.exp(jax.random.uniform(entry_key, full_shape, jnp.float32, jnp.log(0.2), jnp.log(2.0)))
    return (factor * scale[None, None]).astype(jnp.float32)


def wall_layout(key):
    layout_key = jax.random.fold_in(key, 201)
    block_key, count_key, facet_key = jax.random.split(layout_key, 3)
    tile_keys = jax.random.split(block_key, TILES)

    def pick_blocks(one_key):
        return jax.random.permutation(one_key, TILE_BLOCKS)[:WMAX]
    blocks = jax.vmap(pick_blocks)(tile_keys).astype(jnp.int32)
    half_tiles = TILES // 2
    large_key, small_key, force_key, flip_key = jax.random.split(count_key, 4)
    larger = jax.random.randint(large_key, (half_tiles,), WPAIR, WMAX + 1)
    forced = jax.random.randint(force_key, (), 0, half_tiles)
    larger = jnp.where(jnp.arange(half_tiles) == forced, WMAX, larger)
    smaller = jax.random.randint(small_key, (half_tiles,), 0, WMAX - larger + 1)
    flips = jax.random.randint(flip_key, (half_tiles,), 0, 2)
    first_half = jnp.where(flips == 1, larger, smaller)
    second_half = jnp.where(flips == 1, smaller, larger)
    counts = jnp.concatenate([first_half, second_half]).astype(jnp.int32)
    facets = jax.random.randint(facet_key, (TILES, WMAX, BLOCK), 0, 7)
    slot_ids = jnp.arange(WMAX, dtype=jnp.int32)
    facets = jnp.where(slot_ids[None, :, None] < counts[:, None, None], facets, 0).astype(jnp.int32)
    return (blocks, counts, facets)


def draw_wall_blocks(key, part):
    return wall_layout(key)[0]


def draw_wall_count(key, part):
    return wall_layout(key)[1]


def draw_wall_facet(key, part):
    return wall_layout(key)[2]


def setup_inputs(seed: int = 0) -> dict:
    arg_keys = jax.random.split(jax.random.key(seed), 12)
    return {
        "phonon_heat_density": draw_phonon_heat_density(jax.random.fold_in(arg_keys[11], 71), 0),
        "directions": draw_directions(jax.random.fold_in(arg_keys[11], 71), 0),
        "quad_weight": draw_quad_weight(jax.random.fold_in(arg_keys[11], 71), 0),
        "mirror": draw_mirror(jax.random.fold_in(arg_keys[11], 71), 0),
        "band_courant": jnp.clip(jax.random.uniform(arg_keys[4], (BANDS,), jnp.float32, 0.3, 1.9), 0.3, 1.9),
        "relax_rate": jnp.clip(jnp.exp(jax.random.uniform(arg_keys[5], (BANDS,), jnp.float32, math.log(0.05), math.log(0.95))), 0.05, 0.95),
        "mode_heat_magnitude": jnp.clip(jnp.exp(jax.random.uniform(arg_keys[6], (BANDS,), jnp.float32, math.log(0.5), math.log(2.0))), 0.5, 2.0),
        "mode_pulsation": jnp.clip(jnp.exp(jax.random.uniform(arg_keys[7], (BANDS,), jnp.float32, math.log(0.3), math.log(2.5))), 0.3, 2.5),
        "wall_blocks": draw_wall_blocks(jax.random.fold_in(arg_keys[11], 71), 0),
        "wall_count": draw_wall_count(jax.random.fold_in(arg_keys[11], 71), 0),
        "wall_facet": draw_wall_facet(jax.random.fold_in(arg_keys[11], 71), 0),
    }


def beam_coeffs(courant):
    abs_speed = jnp.abs(courant)
    centre = 1.0 - 1.5 * abs_speed + 0.5 * abs_speed * abs_speed
    near_weight = 2.0 * abs_speed - abs_speed * abs_speed
    far_weight = 0.5 * abs_speed * abs_speed - 0.5 * abs_speed
    forward = courant > 0
    return (centre, jnp.where(forward, near_weight, 0.0), jnp.where(forward, far_weight, 0.0),
            jnp.where(forward, 0.0, near_weight), jnp.where(forward, 0.0, far_weight))


def combine(coeffs, centre_field, back_one, back_two, fore_one, fore_two):
    return (coeffs[0] * centre_field + coeffs[1] * back_one + coeffs[2] * back_two
            + coeffs[3] * fore_one + coeffs[4] * fore_two)


def roll_sweep(field_in, coeffs, axis_num):
    return combine(coeffs, field_in, jnp.roll(field_in, 1, axis_num), jnp.roll(field_in, 2, axis_num),
                   jnp.roll(field_in, -1, axis_num), jnp.roll(field_in, -2, axis_num))


def root_finder_guess(injection_contribution, collision_speed_factor, mode_pulsation):
    pseudo_kelvin_field = jnp.ones_like(injection_contribution)
    for newton_turn in range(NEWTON):
        dimensionless_pulsation = mode_pulsation[:, None] / pseudo_kelvin_field[None, :]
        heat_surplus = jnp.expm1(dimensionless_pulsation)
        mismatch_error = jnp.sum(collision_speed_factor[:, None] / heat_surplus, axis=0) - injection_contribution
        gradient_guess = jnp.sum(collision_speed_factor[:, None] * dimensionless_pulsation * jnp.exp(dimensionless_pulsation) / (heat_surplus * heat_surplus), axis=0) / pseudo_kelvin_field
        pseudo_kelvin_field = jnp.clip(pseudo_kelvin_field - mismatch_error / gradient_guess, 0.5 * pseudo_kelvin_field, 2.0 * pseudo_kelvin_field)
    return pseudo_kelvin_field


def reflect_walls(phonon_heat_density, directions, mirror, wall_blocks, wall_count, wall_facet):
    grid_view = phonon_heat_density.reshape(DIRS, BANDS, TILES, TILE_BLOCKS, BLOCK)
    tile_ids = jnp.arange(TILES, dtype=jnp.int32)[:, None]
    walls = grid_view[:, :, tile_ids, wall_blocks]
    slot_ids = jnp.arange(WMAX, dtype=jnp.int32)
    facets = jnp.where(slot_ids[None, :, None] < wall_count[:, None, None], wall_facet, 0)
    result = walls
    for axis_num in range(3):
        mirrored = walls[mirror[axis_num]]
        component = directions[axis_num][:, None, None, None, None]
        chosen = (((facets == 2 * axis_num + 1)[None, None] & (component > 0))
                  | ((facets == 2 * axis_num + 2)[None, None] & (component < 0)))
        result = jnp.where(chosen, mirrored, result)
    grid_view = grid_view.at[:, :, tile_ids, wall_blocks].set(result)
    return grid_view.reshape(phonon_heat_density.shape)


def reference(phonon_heat_density, directions, quad_weight, mirror, band_courant, relax_rate, mode_heat_magnitude, mode_pulsation, wall_blocks, wall_count, wall_facet):
    def move_one(pair):
        field_in, unit_vec = pair
        moved = roll_sweep(field_in, beam_coeffs((unit_vec[0] * band_courant)[:, None, None, None]), 1)
        moved = roll_sweep(moved, beam_coeffs((unit_vec[1] * band_courant)[:, None, None, None]), 3)
        moved = roll_sweep(moved, beam_coeffs((unit_vec[2] * band_courant)[:, None, None, None]), 2)
        return moved

    weights = (quad_weight[:, None] * relax_rate[None, :]).reshape(-1)
    collision_speed_factor = relax_rate * mode_heat_magnitude
    pseudo_kelvin_field = jnp.ones((MESH_WIDE_COUNT * LAYER_HIGH_COUNT * MESH_DEEP_COUNT,), jnp.float32)
    for step_num in range(STEPS):
        phonon_heat_density = reflect_walls(phonon_heat_density, directions, mirror, wall_blocks, wall_count, wall_facet)
        phonon_heat_density = lax.map(move_one, (phonon_heat_density, directions.T))
        injection_contribution = jnp.tensordot(weights, phonon_heat_density.reshape(DIRS * BANDS, MESH_WIDE_COUNT * LAYER_HIGH_COUNT * MESH_DEEP_COUNT), axes=1, precision=lax.Precision.HIGHEST)
        pseudo_kelvin_field = root_finder_guess(injection_contribution, collision_speed_factor, mode_pulsation)
        bose_einstein_heat = mode_heat_magnitude[:, None] / jnp.expm1(mode_pulsation[:, None] / pseudo_kelvin_field[None, :])
        phonon_heat_density = phonon_heat_density + relax_rate[None, :, None, None, None] * (bose_einstein_heat.reshape(1, BANDS, MESH_WIDE_COUNT, LAYER_HIGH_COUNT, MESH_DEEP_COUNT) - phonon_heat_density)
    return phonon_heat_density, pseudo_kelvin_field.reshape(MESH_WIDE_COUNT, LAYER_HIGH_COUNT, MESH_DEEP_COUNT)
```

```python
import functools

import jax
import jax.numpy as jnp
from jax import lax
from jax.experimental import pallas as pl
from jax.experimental.pallas import tpu as pltpu
from jax.sharding import PartitionSpec as P

STEPS = 2
NEWTON = 4
BLOCK = 128
OCT = 8


def pick(values, index):
    hits = index[:, None] == jnp.arange(values.shape[0], dtype=jnp.int32)[None, :]
    return jnp.sum(jnp.where(hits, values[None, :], jnp.zeros((), values.dtype)), axis=1)


def orbit_order(directions, mirror):
    count = directions.shape[1]
    ids = jnp.arange(count, dtype=jnp.int32)
    positive = (directions > 0).astype(jnp.int32)
    code = positive[0] + 2 * positive[1] + 4 * positive[2]
    rep = ids
    for axis_num in range(3):
        flipped = pick(mirror[axis_num], rep)
        rep = jnp.where(positive[axis_num] > 0, rep, flipped)
    is_rep = code == 7
    rank_of_rep = jnp.sum(
        jnp.where(is_rep[None, :] & (ids[None, :] < rep[:, None]), 1, 0), axis=1
    ).astype(jnp.int32)
    position = rank_of_rep * OCT + code
    order = jnp.sum(
        jnp.where(position[None, :] == ids[:, None], ids[None, :], 0), axis=1
    ).astype(jnp.int32)
    return order, position


def facet_grid(wall_blocks, wall_count, wall_facet, tile_blocks):
    slot_ids = jnp.arange(wall_blocks.shape[0], dtype=jnp.int32)
    hits = (wall_blocks[None, :] == jnp.arange(tile_blocks, dtype=jnp.int32)[:, None]) & (
        slot_ids < wall_count
    )[None, :]
    return jnp.sum(jnp.where(hits[:, :, None], wall_facet[None], 0), axis=1).astype(jnp.int32)


def sweep_kernel(high, tiles, relaxed, coef_ref, facet_ref, e_ref, *rest):
    if relaxed:
        bose_ref, moved_ref, source_ref, now_ref = rest
    else:
        moved_ref, source_ref = rest
        now_ref = e_ref
    band, orbit = pl.program_id(0), pl.program_id(1)
    unit = band * pl.num_programs(1) + orbit
    coef = [coef_ref[unit, i] for i in range(10)]
    rows, width = e_ref.shape[3], e_ref.shape[4]
    row_id = lax.broadcasted_iota(jnp.int32, (rows, width), 0)
    lane_id = lax.broadcasted_iota(jnp.int32, (rows, width), 1)
    height = row_id % high

    @pl.when((band == 0) & (orbit == 0))
    def _():
        source_ref[...] = jnp.zeros_like(source_ref)

    def roll(u, by, axis):
        return pltpu.roll(u, by % u.shape[axis], axis)

    if relaxed:
        for t in range(tiles):
            bose = bose_ref[0, t]
            for o in range(OCT):
                u = e_ref[t, o, 0]
                now_ref[t, o, 0] = u + coef_ref[unit, 10] * (bose - u)

    total = [jnp.zeros((rows, width), jnp.float32) for _ in range(tiles)]
    for o in range(OCT):
        way = [1 if o >> a & 1 else -1 for a in range(3)]
        cells = []
        for t in range(tiles):
            facets = facet_ref[t]
            u = now_ref[t, o, 0]
            for a in range(3):
                facing = 2 * a + 1 if way[a] > 0 else 2 * a + 2
                u = jnp.where(facets == facing, now_ref[t, o ^ (1 << a), 0], u)
            cells.append(u)
        turned = [roll(u, high * way[0], 0) for u in cells]
        for t in range(tiles):
            up = (t - way[0]) % tiles
            edge = row_id < high if way[0] > 0 else row_id >= rows - high
            near = jnp.where(edge, turned[up], turned[t])
            u = coef[0] * cells[t] + coef[1] * near + coef[2] * cells[up]
            u = coef[3] * u + coef[4] * roll(u, way[1], 1) + coef[5] * roll(u, 2 * way[1], 1)
            wrap1 = height < 1 if way[2] > 0 else height >= high - 1
            wrap2 = height < 2 if way[2] > 0 else height >= high - 2
            near = jnp.where(wrap1, roll(u, (1 - high) * way[2], 0), roll(u, way[2], 0))
            far = jnp.where(wrap2, roll(u, (2 - high) * way[2], 0), roll(u, 2 * way[2], 0))
            u = coef[6] * u + coef[7] * near + coef[8] * far
            moved_ref[t, o, 0] = u
            total[t] = total[t] + u
    for t in range(tiles):
        source_ref[t] = source_ref[t] + coef[9] * total[t]


def sweep(high, coefs, facets, field, bose):
    tiles, dirs, bands, rows, width = field.shape
    orbits = dirs // OCT
    block = pl.BlockSpec((tiles, OCT, 1, rows, width), lambda b, o: (0, o, b, 0, 0))
    whole = pl.BlockSpec((tiles, rows, width), lambda b, o: (0, 0, 0))
    in_specs = [pl.BlockSpec(memory_space=pltpu.SMEM), whole, block]
    operands = [coefs, facets, field]
    scratch = []
    if bose is not None:
        in_specs.append(pl.BlockSpec((1, tiles, rows, width), lambda b, o: (b, 0, 0, 0)))
        operands.append(bose)
        scratch.append(pltpu.VMEM((tiles, OCT, 1, rows, width), jnp.float32))
    return pl.pallas_call(
        functools.partial(sweep_kernel, high, tiles, bose is not None),
        grid=(bands, orbits),
        in_specs=in_specs,
        out_specs=[block, whole],
        out_shape=[
            jax.ShapeDtypeStruct(field.shape, jnp.float32),
            jax.ShapeDtypeStruct((tiles, rows, width), jnp.float32),
        ],
        scratch_shapes=scratch,
        compiler_params=pltpu.CompilerParams(dimension_semantics=("arbitrary", "arbitrary")),
    )(*operands)


def beam_coeffs(abs_speed):
    return (
        1.0 - 1.5 * abs_speed + 0.5 * abs_speed * abs_speed,
        2.0 * abs_speed - abs_speed * abs_speed,
        0.5 * abs_speed * abs_speed - 0.5 * abs_speed,
    )


def root_finder_guess(injection_contribution, collision_speed_factor, mode_pulsation):
    pseudo_kelvin_field = jnp.ones_like(injection_contribution)
    for newton_turn in range(NEWTON):
        dimensionless_pulsation = mode_pulsation[:, None] / pseudo_kelvin_field[None, :]
        heat_surplus = jnp.expm1(dimensionless_pulsation)
        mismatch_error = (
            jnp.sum(collision_speed_factor[:, None] / heat_surplus, axis=0) - injection_contribution
        )
        gradient_guess = (
            jnp.sum(
                collision_speed_factor[:, None]
                * dimensionless_pulsation
                * jnp.exp(dimensionless_pulsation)
                / (heat_surplus * heat_surplus),
                axis=0,
            )
            / pseudo_kelvin_field
        )
        pseudo_kelvin_field = jnp.clip(
            pseudo_kelvin_field - mismatch_error / gradient_guess,
            0.5 * pseudo_kelvin_field,
            2.0 * pseudo_kelvin_field,
        )
    return pseudo_kelvin_field


def on_device(
    phonon_heat_density,
    directions,
    quad_weight,
    mirror,
    band_courant,
    relax_rate,
    mode_heat_magnitude,
    mode_pulsation,
    wall_blocks,
    wall_count,
    wall_facet,
):
    local_dirs, bands, wide, high, deep = phonon_heat_density.shape
    tiles, groups = lax.axis_size("space"), lax.axis_size("dir")
    tile, group = lax.axis_index("space"), lax.axis_index("dir")
    rows = wide * high
    share = -(-bands // groups)
    extra = share * groups - bands
    dirs = directions.shape[1]
    orbits = dirs // OCT
    part = dirs // tiles
    part_orbits = orbits // tiles

    order, position = orbit_order(directions, mirror)
    own_facets = facet_grid(
        wall_blocks[0], wall_count[0], wall_facet[0], wide * high * deep // BLOCK
    ).astype(jnp.float32)
    facets = lax.all_gather(own_facets.reshape(rows, deep), "space").astype(jnp.int32)

    def own_bands(values):
        return lax.dynamic_slice_in_dim(jnp.pad(values, (0, extra)), group * share, share)

    courant, rates = own_bands(band_courant), own_bands(relax_rate)
    magnitudes = own_bands(mode_heat_magnitude)
    pulsations = lax.dynamic_slice_in_dim(
        jnp.pad(mode_pulsation, (0, extra), constant_values=1.0), group * share, share
    )
    reps = lax.dynamic_slice_in_dim(
        order.reshape(orbits, OCT)[:, OCT - 1], tile * part_orbits, part_orbits
    )
    columns = []
    for axis_num in range(3):
        unit = jnp.abs(pick(directions[axis_num], reps))
        columns.extend(beam_coeffs(courant[:, None] * unit[None, :]))
    columns.append(rates[:, None] * pick(quad_weight, reps)[None, :])
    columns.append(jnp.broadcast_to(rates[:, None], columns[0].shape))
    coefs = jnp.stack(columns, axis=-1).reshape(share * part_orbits, len(columns))

    field = phonon_heat_density.reshape(local_dirs, bands, rows, deep)
    field = jnp.pad(field, ((0, 0), (0, extra), (0, 0), (0, 0)))
    field = lax.all_to_all(field, "dir", split_axis=1, concat_axis=0, tiled=True)
    field = jnp.take(field, order, axis=0, mode="clip")
    field = lax.all_to_all(field, "space", split_axis=0, concat_axis=0, tiled=True)
    field = field.reshape(tiles, part, share, rows, deep)

    collision_speed_factor = relax_rate * mode_heat_magnitude
    bose = None
    for step_num in range(STEPS):
        field, source = sweep(high, coefs, facets, field, bose)
        source = lax.psum(source, ("space", "dir"))
        if step_num < STEPS - 1:
            kelvin = root_finder_guess(
                source.reshape(-1), collision_speed_factor, mode_pulsation
            ).reshape(source.shape)
            bose = magnitudes[:, None, None, None] / jnp.expm1(
                pulsations[:, None, None, None] / kelvin[None]
            )
    own_source = lax.dynamic_index_in_dim(source, tile, 0, keepdims=False)
    kelvin = root_finder_guess(own_source.reshape(-1), collision_speed_factor, mode_pulsation)
    kelvin = kelvin.reshape(wide, high, deep)
    field = field.reshape(dirs, share, rows, deep)
    field = lax.all_to_all(field, "space", split_axis=0, concat_axis=0, tiled=True)
    field = jnp.take(field, position, axis=0, mode="clip")
    field = lax.all_to_all(field, "dir", split_axis=0, concat_axis=1, tiled=True)
    moved = field[:, :bands].reshape(phonon_heat_density.shape)
    home = mode_heat_magnitude[:, None, None, None] / jnp.expm1(
        mode_pulsation[:, None, None, None] / kelvin[None]
    )
    out = moved + relax_rate[None, :, None, None, None] * (home[None] - moved)
    return out, kelvin


def solution(mesh):
    in_specs = (
        P("dir", None, "space", None, None),
        P(),
        P(),
        P(),
        P(),
        P(),
        P(),
        P(),
        P("space", None),
        P("space"),
        P("space", None, None),
    )
    out_specs = (P("dir", None, "space", None, None), P("space", None, None))
    return jax.shard_map(
        on_device, mesh=mesh, in_specs=in_specs, out_specs=out_specs, check_vma=False
    )
```

```python
import functools

import jax
import jax.numpy as jnp
from jax import lax
from jax.experimental import pallas as pl
from jax.experimental.pallas import tpu as pltpu
from jax.sharding import PartitionSpec as P

STEPS = 2
NEWTON = 4
BLOCK = 128
OCT = 8


def pick(values, index):
    hits = index[:, None] == jnp.arange(values.shape[0], dtype=jnp.int32)[None, :]
    return jnp.sum(jnp.where(hits, values[None, :], jnp.zeros((), values.dtype)), axis=1)


def orbit_order(directions, mirror):
    count = directions.shape[1]
    ids = jnp.arange(count, dtype=jnp.int32)
    positive = (directions > 0).astype(jnp.int32)
    code = positive[0] + 2 * positive[1] + 4 * positive[2]
    rep = ids
    for axis_num in range(3):
        flipped = pick(mirror[axis_num], rep)
        rep = jnp.where(positive[axis_num] > 0, rep, flipped)
    is_rep = code == 7
    rank_of_rep = jnp.sum(
        jnp.where(is_rep[None, :] & (ids[None, :] < rep[:, None]), 1, 0), axis=1
    ).astype(jnp.int32)
    position = rank_of_rep * OCT + code
    order = jnp.sum(
        jnp.where(position[None, :] == ids[:, None], ids[None, :], 0), axis=1
    ).astype(jnp.int32)
    return order, position


def facet_grid(wall_blocks, wall_count, wall_facet, tile_blocks):
    slot_ids = jnp.arange(wall_blocks.shape[0], dtype=jnp.int32)
    hits = (wall_blocks[None, :] == jnp.arange(tile_blocks, dtype=jnp.int32)[:, None]) & (
        slot_ids < wall_count
    )[None, :]
    return jnp.sum(jnp.where(hits[:, :, None], wall_facet[None], 0), axis=1).astype(jnp.int32)


def sweep_kernel(high, tiles, relaxed, coef_ref, facet_ref, e_ref, *rest):
    if relaxed:
        bose_ref, moved_ref, source_ref, now_ref = rest
    else:
        moved_ref, source_ref = rest
        now_ref = e_ref
    band, orbit = pl.program_id(0), pl.program_id(1)
    unit = band * pl.num_programs(1) + orbit
    coef = [coef_ref[unit, i] for i in range(10)]
    rows, width = e_ref.shape[3], e_ref.shape[4]
    row_id = lax.broadcasted_iota(jnp.int32, (rows, width), 0)
    lane_id = lax.broadcasted_iota(jnp.int32, (rows, width), 1)
    height = row_id % high

    @pl.when((band == 0) & (orbit == 0))
    def _():
        source_ref[...] = jnp.zeros_like(source_ref)

    def roll(u, by, axis):
        return pltpu.roll(u, by % u.shape[axis], axis)

    if relaxed:
        for t in range(tiles):
            bose = bose_ref[0, t]
            for o in range(OCT):
                u = e_ref[t, o, 0]
                now_ref[t, o, 0] = u + coef_ref[unit, 10] * (bose - u)

    total = [jnp.zeros((rows, width), jnp.float32) for _ in range(tiles)]
    for o in range(OCT):
        way = [1 if o >> a & 1 else -1 for a in range(3)]
        cells = []
        for t in range(tiles):
            facets = facet_ref[t]
            u = now_ref[t, o, 0]
            for a in range(3):
                facing = 2 * a + 1 if way[a] > 0 else 2 * a + 2
                u = jnp.where(facets == facing, now_ref[t, o ^ (1 << a), 0], u)
            cells.append(u)
        turned = [roll(u, high * way[0], 0) for u in cells]
        for t in range(tiles):
            up = (t - way[0]) % tiles
            edge = row_id < high if way[0] > 0 else row_id >= rows - high
            near = jnp.where(edge, turned[up], turned[t])
            u = coef[0] * cells[t] + coef[1] * near + coef[2] * cells[up]
            u = coef[3] * u + coef[4] * roll(u, way[1], 1) + coef[5] * roll(u, 2 * way[1], 1)
            wrap1 = height < 1 if way[2] > 0 else height >= high - 1
            wrap2 = height < 2 if way[2] > 0 else height >= high - 2
            near = jnp.where(wrap1, roll(u, (1 - high) * way[2], 0), roll(u, way[2], 0))
            far = jnp.where(wrap2, roll(u, (2 - high) * way[2], 0), roll(u, 2 * way[2], 0))
            u = coef[6] * u + coef[7] * near + coef[8] * far
            moved_ref[t, o, 0] = u
            total[t] = total[t] + u
    for t in range(tiles):
        source_ref[t] = source_ref[t] + coef[9] * total[t]


def sweep(high, coefs, facets, field, bose):
    tiles, dirs, bands, rows, width = field.shape
    orbits = dirs // OCT
    block = pl.BlockSpec((tiles, OCT, 1, rows, width), lambda b, o: (0, o, b, 0, 0))
    whole = pl.BlockSpec((tiles, rows, width), lambda b, o: (0, 0, 0))
    in_specs = [pl.BlockSpec(memory_space=pltpu.SMEM), whole, block]
    operands = [coefs, facets, field]
    scratch = []
    if bose is not None:
        in_specs.append(pl.BlockSpec((1, tiles, rows, width), lambda b, o: (b, 0, 0, 0)))
        operands.append(bose)
        scratch.append(pltpu.VMEM((tiles, OCT, 1, rows, width), jnp.float32))
    return pl.pallas_call(
        functools.partial(sweep_kernel, high, tiles, bose is not None),
        grid=(bands, orbits),
        in_specs=in_specs,
        out_specs=[block, whole],
        out_shape=[
            jax.ShapeDtypeStruct(field.shape, jnp.float32),
            jax.ShapeDtypeStruct((tiles, rows, width), jnp.float32),
        ],
        scratch_shapes=scratch,
        compiler_params=pltpu.CompilerParams(dimension_semantics=("arbitrary", "arbitrary")),
    )(*operands)


MESH = pl.DeviceIdType.MESH


def greet(tile, tiles, group, groups):
    barrier = pltpu.get_barrier_semaphore()
    for u in range(1, tiles):
        pl.semaphore_signal(
            barrier, inc=1, device_id=(lax.rem(tile + u, tiles), group), device_id_type=MESH
        )
    for t in range(1, groups):
        pl.semaphore_signal(
            barrier, inc=1, device_id=(tile, lax.rem(group + t, groups)), device_id_type=MESH
        )
    pl.semaphore_wait(barrier, tiles + groups - 2)


def remote(src, dst, send, recv, device):
    return pltpu.make_async_remote_copy(
        src_ref=src, dst_ref=dst, send_sem=send, recv_sem=recv, device_id=device, device_id_type=MESH
    )


def spread_kernel(
    tiles, groups, order_ref, facet_ref, home_ref, field_ref, facets_ref, *scratch
):
    share = field_ref.shape[2]
    landed, sorted_refs = scratch[:share], scratch[share : 2 * share]
    dir_send, dir_recv, tile_send, tile_recv, facet_send, facet_recv, own_sem = scratch[2 * share :]
    local_dirs, _, wide, high, _ = home_ref.shape
    dirs, part = landed[0].shape[0], field_ref.shape[1]
    tile, group = lax.axis_index("space"), lax.axis_index("dir")

    own = [
        pltpu.make_async_copy(
            home_ref.at[:, group * share + k],
            landed[k].at[pl.ds(group * local_dirs, local_dirs)],
            own_sem.at[k],
        )
        for k in range(share)
    ]
    for copy in own:
        copy.start()
    own_facets = pltpu.make_async_copy(facet_ref, facets_ref.at[tile], own_sem.at[2 * share])
    own_facets.start()
    greet(tile, tiles, group, groups)

    first = []
    for k in range(share):
        line = []
        for t in range(1, groups):
            peer = lax.rem(group + t, groups)
            copy = remote(
                home_ref.at[:, peer * share + k],
                landed[k].at[pl.ds(group * local_dirs, local_dirs)],
                dir_send.at[k, t],
                dir_recv.at[k, t],
                (tile, peer),
            )
            copy.start()
            line.append(copy)
        first.append(line)
    third = []
    for u in range(1, tiles):
        copy = remote(
            facet_ref,
            facets_ref.at[tile],
            facet_send.at[u],
            facet_recv.at[u],
            (lax.rem(tile + u, tiles), group),
        )
        copy.start()
        third.append(copy)

    second, kept = [], []
    for k in range(share):
        own[k].wait()
        for copy in first[k]:
            copy.wait_recv()

        def move(j, carry):
            d = order_ref[j]
            for x in range(wide):
                sorted_refs[k][j, x * high : (x + 1) * high, :] = landed[k][d, x]
            return carry

        lax.fori_loop(0, dirs, move, 0, unroll=4)
        for u in range(1, tiles):
            peer = lax.rem(tile + u, tiles)
            copy = remote(
                sorted_refs[k].at[pl.ds(peer * part, part)],
                field_ref.at[tile, :, k],
                tile_send.at[k, u],
                tile_recv.at[k, u],
                (peer, group),
            )
            copy.start()
            second.append(copy)
        copy = pltpu.make_async_copy(
            sorted_refs[k].at[pl.ds(tile * part, part)],
            field_ref.at[tile, :, k],
            own_sem.at[share + k],
        )
        copy.start()
        kept.append(copy)
    own_facets.wait()
    for copy in kept:
        copy.wait()
    for copy in second + third:
        copy.wait_recv()
    for line in first:
        for copy in line:
            copy.wait_send()
    for copy in second + third:
        copy.wait_send()


def spread(tiles, groups, share, order, facets, home):
    local_dirs, _, wide, high, deep = home.shape
    dirs, rows = local_dirs * groups, wide * high
    part = dirs // tiles
    vmem = pl.BlockSpec(memory_space=pltpu.VMEM)
    anywhere = pl.BlockSpec(memory_space=pl.ANY)
    dma = pltpu.SemaphoreType.DMA
    return pl.pallas_call(
        functools.partial(spread_kernel, tiles, groups),
        in_specs=[pl.BlockSpec(memory_space=pltpu.SMEM), vmem, anywhere],
        out_specs=[anywhere, vmem],
        out_shape=[
            jax.ShapeDtypeStruct((tiles, part, share, rows, deep), jnp.float32),
            jax.ShapeDtypeStruct((tiles, rows, deep), jnp.float32),
        ],
        scratch_shapes=[pltpu.VMEM((dirs, wide, high, deep), jnp.float32)] * share
        + [pltpu.VMEM((dirs, rows, deep), jnp.float32)] * share
        + [
            dma((share, groups)),
            dma((share, groups)),
            dma((share, tiles)),
            dma((share, tiles)),
            dma((tiles,)),
            dma((tiles,)),
            dma((2 * share + 1,)),
        ],
        compiler_params=pltpu.CompilerParams(collective_id=0, has_side_effects=True),
    )(order, facets, home)


def collect_kernel(tiles, groups, position_ref, field_ref, home_ref, *scratch):
    share = field_ref.shape[2]
    landed, sorted_refs = scratch[:share], scratch[share : 2 * share]
    dir_send, dir_recv, tile_send, tile_recv, own_sem = scratch[2 * share :]
    local_dirs, _, wide, high, _ = home_ref.shape
    dirs, part = landed[0].shape[0], field_ref.shape[1]
    tile, group = lax.axis_index("space"), lax.axis_index("dir")
    own = [
        pltpu.make_async_copy(
            field_ref.at[tile, :, k], landed[k].at[pl.ds(tile * part, part)], own_sem.at[k]
        )
        for k in range(share)
    ]
    for copy in own:
        copy.start()
    greet(tile, tiles, group, groups)
    first = []
    for k in range(share):
        line = []
        for u in range(1, tiles):
            peer = lax.rem(tile + u, tiles)
            copy = remote(
                field_ref.at[peer, :, k],
                landed[k].at[pl.ds(tile * part, part)],
                tile_send.at[k, u],
                tile_recv.at[k, u],
                (peer, group),
            )
            copy.start()
            line.append(copy)
        first.append(line)
    second, kept = [], []
    for k in range(share):
        own[k].wait()
        for copy in first[k]:
            copy.wait_recv()

        def move(d, carry):
            j = position_ref[d]
            for x in range(wide):
                sorted_refs[k][d, x] = landed[k][j, x * high : (x + 1) * high, :]
            return carry

        lax.fori_loop(0, dirs, move, 0, unroll=4)
        for t in range(1, groups):
            peer = lax.rem(group + t, groups)
            copy = remote(
                sorted_refs[k].at[pl.ds(peer * local_dirs, local_dirs)],
                home_ref.at[:, group * share + k],
                dir_send.at[k, t],
                dir_recv.at[k, t],
                (tile, peer),
            )
            copy.start()
            second.append(copy)
        copy = pltpu.make_async_copy(
            sorted_refs[k].at[pl.ds(group * local_dirs, local_dirs)],
            home_ref.at[:, group * share + k],
            own_sem.at[share + k],
        )
        copy.start()
        kept.append(copy)
    for copy in kept:
        copy.wait()
    for copy in second:
        copy.wait_recv()
    for line in first:
        for copy in line:
            copy.wait_send()
    for copy in second:
        copy.wait_send()


def collect(tiles, groups, position, field, high):
    _, part, share, rows, deep = field.shape
    dirs = part * tiles
    local_dirs, wide = dirs // groups, rows // high
    anywhere = pl.BlockSpec(memory_space=pl.ANY)
    dma = pltpu.SemaphoreType.DMA
    return pl.pallas_call(
        functools.partial(collect_kernel, tiles, groups),
        in_specs=[pl.BlockSpec(memory_space=pltpu.SMEM), anywhere],
        out_specs=anywhere,
        out_shape=jax.ShapeDtypeStruct(
            (local_dirs, share * groups, wide, high, deep), jnp.float32
        ),
        scratch_shapes=[pltpu.VMEM((dirs, rows, deep), jnp.float32)] * share
        + [pltpu.VMEM((dirs, wide, high, deep), jnp.float32)] * share
        + [
            dma((share, groups)),
            dma((share, groups)),
            dma((share, tiles)),
            dma((share, tiles)),
            dma((2 * share,)),
        ],
        compiler_params=pltpu.CompilerParams(collective_id=1, has_side_effects=True),
    )(position, field)


def total_kernel(tiles, groups, everywhere, part_ref, total_ref, near, own, far, summed, *sems):
    near_send, near_recv, far_send, far_recv, last_send, last_recv = sems
    tile, group = lax.axis_index("space"), lax.axis_index("dir")
    greet(tile, tiles, group, groups)
    copies = []
    for u in range(1, tiles):
        peer = lax.rem(tile + u, tiles)
        copy = remote(
            part_ref.at[peer], near.at[u], near_send.at[u], near_recv.at[u], (peer, group)
        )
        copy.start()
        copies.append(copy)
    value = part_ref[tile]
    for u in range(1, tiles):
        copies[u - 1].wait_recv()
        value = value + near[u]
    own[...] = value
    gathers = []
    for t in range(1, groups):
        peer = lax.rem(group + t, groups)
        copy = remote(own, far.at[group], far_send.at[t], far_recv.at[t], (tile, peer))
        copy.start()
        gathers.append(copy)
    far[group] = value
    for copy in gathers:
        copy.wait_recv()
    value = far[0]
    for g in range(1, groups):
        value = value + far[g]
    lasts = []
    if everywhere:
        summed[...] = value
        for u in range(1, tiles):
            peer = lax.rem(tile + u, tiles)
            copy = remote(
                summed, total_ref.at[tile], last_send.at[u], last_recv.at[u], (peer, group)
            )
            copy.start()
            lasts.append(copy)
        total_ref[tile] = value
        for copy in lasts:
            copy.wait_recv()
    else:
        total_ref[0] = value
    for copy in copies + gathers + lasts:
        copy.wait_send()


def total(tiles, groups, everywhere, source):
    _, rows, deep = source.shape
    vmem = pl.BlockSpec(memory_space=pltpu.VMEM)
    dma = pltpu.SemaphoreType.DMA
    return pl.pallas_call(
        functools.partial(total_kernel, tiles, groups, everywhere),
        in_specs=[vmem],
        out_specs=vmem,
        out_shape=jax.ShapeDtypeStruct((tiles if everywhere else 1, rows, deep), jnp.float32),
        scratch_shapes=[
            pltpu.VMEM((tiles, rows, deep), jnp.float32),
            pltpu.VMEM((rows, deep), jnp.float32),
            pltpu.VMEM((groups, rows, deep), jnp.float32),
            pltpu.VMEM((rows, deep), jnp.float32),
            dma((tiles,)),
            dma((tiles,)),
            dma((groups,)),
            dma((groups,)),
            dma((tiles,)),
            dma((tiles,)),
        ],
        compiler_params=pltpu.CompilerParams(
            collective_id=2 if everywhere else 3, has_side_effects=True
        ),
    )(source)


def beam_coeffs(abs_speed):
    return (
        1.0 - 1.5 * abs_speed + 0.5 * abs_speed * abs_speed,
        2.0 * abs_speed - abs_speed * abs_speed,
        0.5 * abs_speed * abs_speed - 0.5 * abs_speed,
    )


def root_finder_guess(injection_contribution, collision_speed_factor, mode_pulsation):
    pseudo_kelvin_field = jnp.ones_like(injection_contribution)
    for newton_turn in range(NEWTON):
        dimensionless_pulsation = mode_pulsation[:, None] / pseudo_kelvin_field[None, :]
        heat_surplus = jnp.expm1(dimensionless_pulsation)
        mismatch_error = (
            jnp.sum(collision_speed_factor[:, None] / heat_surplus, axis=0) - injection_contribution
        )
        gradient_guess = (
            jnp.sum(
                collision_speed_factor[:, None]
                * dimensionless_pulsation
                * jnp.exp(dimensionless_pulsation)
                / (heat_surplus * heat_surplus),
                axis=0,
            )
            / pseudo_kelvin_field
        )
        pseudo_kelvin_field = jnp.clip(
            pseudo_kelvin_field - mismatch_error / gradient_guess,
            0.5 * pseudo_kelvin_field,
            2.0 * pseudo_kelvin_field,
        )
    return pseudo_kelvin_field


def on_device(
    phonon_heat_density,
    directions,
    quad_weight,
    mirror,
    band_courant,
    relax_rate,
    mode_heat_magnitude,
    mode_pulsation,
    wall_blocks,
    wall_count,
    wall_facet,
):
    local_dirs, bands, wide, high, deep = phonon_heat_density.shape
    tiles, groups = lax.axis_size("space"), lax.axis_size("dir")
    tile, group = lax.axis_index("space"), lax.axis_index("dir")
    rows = wide * high
    share = -(-bands // groups)
    extra = share * groups - bands
    dirs = directions.shape[1]
    orbits = dirs // OCT
    part = dirs // tiles
    part_orbits = orbits // tiles

    order, position = orbit_order(directions, mirror)
    own_facets = facet_grid(
        wall_blocks[0], wall_count[0], wall_facet[0], wide * high * deep // BLOCK
    ).astype(jnp.float32)
    def own_bands(values):
        return lax.dynamic_slice_in_dim(jnp.pad(values, (0, extra)), group * share, share)

    courant, rates = own_bands(band_courant), own_bands(relax_rate)
    magnitudes = own_bands(mode_heat_magnitude)
    pulsations = lax.dynamic_slice_in_dim(
        jnp.pad(mode_pulsation, (0, extra), constant_values=1.0), group * share, share
    )
    reps = lax.dynamic_slice_in_dim(
        order.reshape(orbits, OCT)[:, OCT - 1], tile * part_orbits, part_orbits
    )
    columns = []
    for axis_num in range(3):
        unit = jnp.abs(pick(directions[axis_num], reps))
        columns.extend(beam_coeffs(courant[:, None] * unit[None, :]))
    columns.append(rates[:, None] * pick(quad_weight, reps)[None, :])
    columns.append(jnp.broadcast_to(rates[:, None], columns[0].shape))
    coefs = jnp.stack(columns, axis=-1).reshape(share * part_orbits, len(columns))

    home = phonon_heat_density
    if extra:
        home = jnp.pad(home, ((0, 0), (0, extra), (0, 0), (0, 0), (0, 0)))
    field, facets = spread(tiles, groups, share, order, own_facets.reshape(rows, deep), home)
    facets = facets.astype(jnp.int32)

    collision_speed_factor = relax_rate * mode_heat_magnitude
    bose = None
    for step_num in range(STEPS):
        field, source = sweep(high, coefs, facets, field, bose)
        source = total(tiles, groups, step_num < STEPS - 1, source)
        if step_num < STEPS - 1:
            kelvin = root_finder_guess(
                source.reshape(-1), collision_speed_factor, mode_pulsation
            ).reshape(source.shape)
            bose = magnitudes[:, None, None, None] / jnp.expm1(
                pulsations[:, None, None, None] / kelvin[None]
            )
    kelvin = root_finder_guess(source.reshape(-1), collision_speed_factor, mode_pulsation)
    kelvin = kelvin.reshape(wide, high, deep)
    moved = collect(tiles, groups, position, field, high)[:, :bands]
    home = mode_heat_magnitude[:, None, None, None] / jnp.expm1(
        mode_pulsation[:, None, None, None] / kelvin[None]
    )
    out = moved + relax_rate[None, :, None, None, None] * (home[None] - moved)
    return out, kelvin


def solution(mesh):
    in_specs = (
        P("dir", None, "space", None, None),
        P(),
        P(),
        P(),
        P(),
        P(),
        P(),
        P(),
        P("space", None),
        P("space"),
        P("space", None, None),
    )
    out_specs = (P("dir", None, "space", None, None), P("space", None, None))
    return jax.shard_map(
        on_device, mesh=mesh, in_specs=in_specs, out_specs=out_specs, check_vma=False
    )
```

```python
import functools

import jax
import jax.numpy as jnp
from jax import lax
from jax.experimental import pallas as pl
from jax.experimental.pallas import tpu as pltpu
from jax.sharding import PartitionSpec as P

NEWTON = 4
BLOCK = 128
OCT = 8


def pick(values, index):
    hits = index[:, None] == jnp.arange(values.shape[0], dtype=jnp.int32)[None, :]
    return jnp.sum(jnp.where(hits, values[None, :], jnp.zeros((), values.dtype)), axis=1)


def orbit_order(directions, mirror):
    count = directions.shape[1]
    ids = jnp.arange(count, dtype=jnp.int32)
    positive = (directions > 0).astype(jnp.int32)
    code = positive[0] + 2 * positive[1] + 4 * positive[2]
    rep = ids
    for axis_num in range(3):
        flipped = pick(mirror[axis_num], rep)
        rep = jnp.where(positive[axis_num] > 0, rep, flipped)
    is_rep = code == 7
    rank_of_rep = jnp.sum(
        jnp.where(is_rep[None, :] & (ids[None, :] < rep[:, None]), 1, 0), axis=1
    ).astype(jnp.int32)
    position = rank_of_rep * OCT + code
    order = jnp.sum(
        jnp.where(position[None, :] == ids[:, None], ids[None, :], 0), axis=1
    ).astype(jnp.int32)
    return order, position


def facet_grid(wall_blocks, wall_count, wall_facet, tile_blocks):
    slot_ids = jnp.arange(wall_blocks.shape[0], dtype=jnp.int32)
    hits = (wall_blocks[None, :] == jnp.arange(tile_blocks, dtype=jnp.int32)[:, None]) & (
        slot_ids < wall_count
    )[None, :]
    return jnp.sum(jnp.where(hits[:, :, None], wall_facet[None], 0), axis=1).astype(jnp.int32)


def roll(u, by, axis):
    return pltpu.roll(u, by % u.shape[axis], axis)


def sweep_unit(high, tiles, coef_ref, unit, facets_ref, load, store):
    coef = [coef_ref[unit, i] for i in range(10)]
    _, rows, width = facets_ref.shape
    row_id = lax.broadcasted_iota(jnp.int32, (rows, width), 0)
    height = row_id % high
    total = [jnp.zeros((rows, width), jnp.float32) for _ in range(tiles)]
    for o in range(OCT):
        way = [1 if o >> a & 1 else -1 for a in range(3)]
        cells = []
        for t in range(tiles):
            facets = facets_ref[t]
            u = load(t, o)
            for a in range(3):
                facing = float(2 * a + 1 if way[a] > 0 else 2 * a + 2)
                u = jnp.where(facets == facing, load(t, o ^ (1 << a)), u)
            cells.append(u)
        turned = [roll(u, high * way[0], 0) for u in cells]
        for t in range(tiles):
            up = (t - way[0]) % tiles
            edge = row_id < high if way[0] > 0 else row_id >= rows - high
            near = jnp.where(edge, turned[up], turned[t])
            u = coef[0] * cells[t] + coef[1] * near + coef[2] * cells[up]
            u = coef[3] * u + coef[4] * roll(u, way[1], 1) + coef[5] * roll(u, 2 * way[1], 1)
            wrap1 = height < 1 if way[2] > 0 else height >= high - 1
            wrap2 = height < 2 if way[2] > 0 else height >= high - 2
            near = jnp.where(wrap1, roll(u, (1 - high) * way[2], 0), roll(u, way[2], 0))
            far = jnp.where(wrap2, roll(u, (2 - high) * way[2], 0), roll(u, 2 * way[2], 0))
            u = coef[6] * u + coef[7] * near + coef[8] * far
            store(t, o, u)
            total[t] = total[t] + u
    return [coef[9] * total[t] for t in range(tiles)]


MESH = pl.DeviceIdType.MESH


def greet(tile, tiles, group, groups):
    barrier = pltpu.get_barrier_semaphore()
    for u in range(1, tiles):
        pl.semaphore_signal(
            barrier, inc=1, device_id=(lax.rem(tile + u, tiles), group), device_id_type=MESH
        )
    for t in range(1, groups):
        pl.semaphore_signal(
            barrier, inc=1, device_id=(tile, lax.rem(group + t, groups)), device_id_type=MESH
        )
    pl.semaphore_wait(barrier, tiles + groups - 2)


def remote(src, dst, send, recv, device):
    return pltpu.make_async_remote_copy(
        src_ref=src, dst_ref=dst, send_sem=send, recv_sem=recv, device_id=device, device_id_type=MESH
    )


CUTS = 2


def spread_kernel(
    tiles, groups, order_ref, coef_ref, facet_ref, home_ref, moved_ref, source_ref, facets_ref, *scratch
):
    _, part, share, rows, deep = moved_ref.shape
    chunks = share * CUTS
    width = deep // CUTS
    landed, sorted_refs = scratch[:chunks], scratch[chunks : 2 * chunks]
    fields = scratch[2 * chunks : 2 * chunks + share]
    dir_send, dir_recv, tile_send, tile_recv, facet_send, facet_recv, own_sem = scratch[
        2 * chunks + share :
    ]
    local_dirs, _, wide, high, _ = home_ref.shape
    dirs, orbits = landed[0].shape[0], part // OCT
    tile, group = lax.axis_index("space"), lax.axis_index("dir")

    def lanes(c):
        return pl.ds(c % CUTS * width, width)

    own = [
        pltpu.make_async_copy(
            home_ref.at[:, group * share + c // CUTS, :, :, lanes(c)],
            landed[c].at[pl.ds(group * local_dirs, local_dirs)],
            own_sem.at[c],
        )
        for c in range(chunks)
    ]
    for copy in own:
        copy.start()
    own_facets = pltpu.make_async_copy(facet_ref, facets_ref.at[tile], own_sem.at[2 * chunks])
    own_facets.start()
    greet(tile, tiles, group, groups)

    third = []
    for u in range(1, tiles):
        copy = remote(
            facet_ref,
            facets_ref.at[tile],
            facet_send.at[u],
            facet_recv.at[u],
            (lax.rem(tile + u, tiles), group),
        )
        copy.start()
        third.append(copy)
    first = []
    for c in range(chunks):
        line = []
        for t in range(1, groups):
            peer = lax.rem(group + t, groups)
            copy = remote(
                home_ref.at[:, peer * share + c // CUTS, :, :, lanes(c)],
                landed[c].at[pl.ds(group * local_dirs, local_dirs)],
                dir_send.at[c, t],
                dir_recv.at[c, t],
                (tile, peer),
            )
            copy.start()
            line.append(copy)
        first.append(line)

    second = []
    source_ref[...] = jnp.zeros_like(source_ref)

    def sweep_band(k):
        for c in range(k * CUTS, (k + 1) * CUTS):
            second[c][0].wait()
            for copy in second[c][1:]:
                copy.wait_recv()

        def one(orbit, carry):
            def store(t, o, u):
                moved_ref[t, orbit * OCT + o, k] = u

            sums = sweep_unit(
                high,
                tiles,
                coef_ref,
                k * orbits + orbit,
                facets_ref,
                lambda t, o: fields[k][t, orbit * OCT + o],
                store,
            )
            for t in range(tiles):
                source_ref[t] = source_ref[t] + sums[t]
            return carry

        lax.fori_loop(0, orbits, one, 0)

    for c in range(chunks):
        own[c].wait()
        for copy in first[c]:
            copy.wait_recv()

        def move(j, carry):
            d = order_ref[j]
            for x in range(wide):
                sorted_refs[c][j, x * high : (x + 1) * high, :] = landed[c][d, x]
            return carry

        lax.fori_loop(0, dirs, move, 0, unroll=4)
        line = [
            pltpu.make_async_copy(
                sorted_refs[c].at[pl.ds(tile * part, part)],
                fields[c // CUTS].at[tile, :, :, lanes(c)],
                own_sem.at[chunks + c],
            )
        ]
        for u in range(1, tiles):
            peer = lax.rem(tile + u, tiles)
            line.append(
                remote(
                    sorted_refs[c].at[pl.ds(peer * part, part)],
                    fields[c // CUTS].at[tile, :, :, lanes(c)],
                    tile_send.at[c, u],
                    tile_recv.at[c, u],
                    (peer, group),
                )
            )
        for copy in line:
            copy.start()
        second.append(line)
        if c == 0:
            own_facets.wait()
            for copy in third:
                copy.wait_recv()
        if c >= CUTS and c % CUTS == 0:
            sweep_band(c // CUTS - 1)
    sweep_band(share - 1)
    for line in first:
        for copy in line:
            copy.wait_send()
    for line in second:
        for copy in line[1:]:
            copy.wait_send()
    for copy in third:
        copy.wait_send()


def spread(tiles, groups, share, order, coefs, facets, home):
    local_dirs, _, wide, high, deep = home.shape
    dirs, rows = local_dirs * groups, wide * high
    part = dirs // tiles
    chunks, width = share * CUTS, deep // CUTS
    vmem = pl.BlockSpec(memory_space=pltpu.VMEM)
    smem = pl.BlockSpec(memory_space=pltpu.SMEM)
    dma = pltpu.SemaphoreType.DMA
    return pl.pallas_call(
        functools.partial(spread_kernel, tiles, groups),
        in_specs=[smem, smem, vmem, pl.BlockSpec(memory_space=pl.ANY)],
        out_specs=[vmem, vmem, vmem],
        out_shape=[
            jax.ShapeDtypeStruct((tiles, part, share, rows, deep), jnp.float32),
            jax.ShapeDtypeStruct((tiles, rows, deep), jnp.float32),
            jax.ShapeDtypeStruct((tiles, rows, deep), jnp.float32),
        ],
        scratch_shapes=[pltpu.VMEM((dirs, wide, high, width), jnp.float32)] * chunks
        + [pltpu.VMEM((dirs, rows, width), jnp.float32)] * chunks
        + [pltpu.VMEM((tiles, part, rows, deep), jnp.float32)] * share
        + [
            dma((chunks, groups)),
            dma((chunks, groups)),
            dma((chunks, tiles)),
            dma((chunks, tiles)),
            dma((tiles,)),
            dma((tiles,)),
            dma((2 * chunks + 1,)),
        ],
        compiler_params=pltpu.CompilerParams(collective_id=0, has_side_effects=True),
    )(order, coefs, facets, home)


def collect_kernel(
    tiles, groups, position_ref, coef_ref, facets_ref, field_ref, bose_ref, home_ref, total_ref, *scratch
):
    _, part, share, rows, deep = field_ref.shape
    chunks = share * CUTS
    width = deep // CUTS
    landed, sorted_refs = scratch[:chunks], scratch[chunks : 2 * chunks]
    swept = scratch[2 * chunks : 2 * chunks + share]
    now_ref, source_ref, near, summed, far = scratch[2 * chunks + share : 2 * chunks + share + 5]
    dir_send, dir_recv, tile_send, tile_recv, near_send, near_recv, far_send, far_recv, own_sem = (
        scratch[2 * chunks + share + 5 :]
    )
    local_dirs, _, wide, high, _ = home_ref.shape
    dirs, orbits = part * tiles, part // OCT
    tile, group = lax.axis_index("space"), lax.axis_index("dir")
    greet(tile, tiles, group, groups)
    source_ref[...] = jnp.zeros_like(source_ref)
    first = []
    for k in range(share):

        def one(orbit, carry):
            unit = k * orbits + orbit
            for t in range(tiles):
                bose = bose_ref[k, t]
                for o in range(OCT):
                    u = field_ref[t, orbit * OCT + o, k]
                    now_ref[t, o] = u + coef_ref[unit, 10] * (bose - u)

            def store(t, o, u):
                swept[k][t, orbit * OCT + o] = u

            sums = sweep_unit(
                high, tiles, coef_ref, unit, facets_ref, lambda t, o: now_ref[t, o], store
            )
            for t in range(tiles):
                source_ref[t] = source_ref[t] + sums[t]
            return carry

        lax.fori_loop(0, orbits, one, 0)
        for c in range(k * CUTS, (k + 1) * CUTS):
            lanes = pl.ds(c % CUTS * width, width)
            line = [
                pltpu.make_async_copy(
                    swept[k].at[tile, :, :, lanes],
                    landed[c].at[pl.ds(tile * part, part)],
                    own_sem.at[c],
                )
            ]
            for u in range(1, tiles):
                peer = lax.rem(tile + u, tiles)
                line.append(
                    remote(
                        swept[k].at[peer, :, :, lanes],
                        landed[c].at[pl.ds(tile * part, part)],
                        tile_send.at[c, u],
                        tile_recv.at[c, u],
                        (peer, group),
                    )
                )
            for copy in line:
                copy.start()
            first.append(line)
    nears = []
    for u in range(1, tiles):
        peer = lax.rem(tile + u, tiles)
        copy = remote(
            source_ref.at[peer], near.at[u], near_send.at[u], near_recv.at[u], (peer, group)
        )
        copy.start()
        nears.append(copy)
    second, fars = [], []
    for c in range(chunks):
        first[c][0].wait()
        for copy in first[c][1:]:
            copy.wait_recv()

        def move(d, carry):
            j = position_ref[d]
            for x in range(wide):
                sorted_refs[c][d, x] = landed[c][j, x * high : (x + 1) * high, :]
            return carry

        lax.fori_loop(0, dirs, move, 0, unroll=4)
        lanes = pl.ds(c % CUTS * width, width)
        line = [
            pltpu.make_async_copy(
                sorted_refs[c].at[pl.ds(group * local_dirs, local_dirs)],
                home_ref.at[:, group * share + c // CUTS, :, :, lanes],
                own_sem.at[chunks + c],
            )
        ]
        for t in range(1, groups):
            peer = lax.rem(group + t, groups)
            line.append(
                remote(
                    sorted_refs[c].at[pl.ds(peer * local_dirs, local_dirs)],
                    home_ref.at[:, group * share + c // CUTS, :, :, lanes],
                    dir_send.at[c, t],
                    dir_recv.at[c, t],
                    (tile, peer),
                )
            )
        for copy in line:
            copy.start()
        second.append(line)
        if c == chunks - 1:
            value = source_ref[tile]
            for u in range(1, tiles):
                nears[u - 1].wait_recv()
                value = value + near[u]
            summed[...] = value
            for t in range(1, groups):
                peer = lax.rem(group + t, groups)
                copy = remote(summed, far.at[group], far_send.at[t], far_recv.at[t], (tile, peer))
                copy.start()
                fars.append(copy)
            far[group] = value
    for line in second:
        line[0].wait()
        for copy in line[1:]:
            copy.wait_recv()
    for copy in fars:
        copy.wait_recv()
    value = far[0]
    for g in range(1, groups):
        value = value + far[g]
    total_ref[...] = value
    for line in first + second:
        for copy in line[1:]:
            copy.wait_send()
    for copy in nears + fars:
        copy.wait_send()


def collect(tiles, groups, position, coefs, facets, field, bose, high):
    _, part, share, rows, deep = field.shape
    dirs = part * tiles
    local_dirs, wide = dirs // groups, rows // high
    chunks, width = share * CUTS, deep // CUTS
    vmem = pl.BlockSpec(memory_space=pltpu.VMEM)
    smem = pl.BlockSpec(memory_space=pltpu.SMEM)
    dma = pltpu.SemaphoreType.DMA
    return pl.pallas_call(
        functools.partial(collect_kernel, tiles, groups),
        in_specs=[smem, smem, vmem, vmem, vmem],
        out_specs=[pl.BlockSpec(memory_space=pl.ANY), vmem],
        out_shape=[
            jax.ShapeDtypeStruct((local_dirs, share * groups, wide, high, deep), jnp.float32),
            jax.ShapeDtypeStruct((rows, deep), jnp.float32),
        ],
        scratch_shapes=[pltpu.VMEM((dirs, rows, width), jnp.float32)] * chunks
        + [pltpu.VMEM((dirs, wide, high, width), jnp.float32)] * chunks
        + [pltpu.VMEM((tiles, part, rows, deep), jnp.float32)] * share
        + [
            pltpu.VMEM((tiles, OCT, rows, deep), jnp.float32),
            pltpu.VMEM((tiles, rows, deep), jnp.float32),
            pltpu.VMEM((tiles, rows, deep), jnp.float32),
            pltpu.VMEM((rows, deep), jnp.float32),
            pltpu.VMEM((groups, rows, deep), jnp.float32),
            dma((chunks, groups)),
            dma((chunks, groups)),
            dma((chunks, tiles)),
            dma((chunks, tiles)),
            dma((tiles,)),
            dma((tiles,)),
            dma((groups,)),
            dma((groups,)),
            dma((2 * chunks,)),
        ],
        compiler_params=pltpu.CompilerParams(collective_id=1, has_side_effects=True),
    )(position, coefs, facets, field, bose)


def total_kernel(tiles, groups, part_ref, total_ref, near, own, far, summed, *sems):
    near_send, near_recv, far_send, far_recv, last_send, last_recv = sems
    tile, group = lax.axis_index("space"), lax.axis_index("dir")
    greet(tile, tiles, group, groups)
    copies = []
    for u in range(1, tiles):
        peer = lax.rem(tile + u, tiles)
        copy = remote(
            part_ref.at[peer], near.at[u], near_send.at[u], near_recv.at[u], (peer, group)
        )
        copy.start()
        copies.append(copy)
    value = part_ref[tile]
    for u in range(1, tiles):
        copies[u - 1].wait_recv()
        value = value + near[u]
    own[...] = value
    gathers = []
    for t in range(1, groups):
        peer = lax.rem(group + t, groups)
        copy = remote(own, far.at[group], far_send.at[t], far_recv.at[t], (tile, peer))
        copy.start()
        gathers.append(copy)
    far[group] = value
    for copy in gathers:
        copy.wait_recv()
    value = far[0]
    for g in range(1, groups):
        value = value + far[g]
    lasts = []
    summed[...] = value
    for u in range(1, tiles):
        peer = lax.rem(tile + u, tiles)
        copy = remote(summed, total_ref.at[tile], last_send.at[u], last_recv.at[u], (peer, group))
        copy.start()
        lasts.append(copy)
    total_ref[tile] = value
    for copy in lasts:
        copy.wait_recv()
    for copy in copies + gathers + lasts:
        copy.wait_send()


def total(tiles, groups, source):
    _, rows, deep = source.shape
    vmem = pl.BlockSpec(memory_space=pltpu.VMEM)
    dma = pltpu.SemaphoreType.DMA
    return pl.pallas_call(
        functools.partial(total_kernel, tiles, groups),
        in_specs=[vmem],
        out_specs=vmem,
        out_shape=jax.ShapeDtypeStruct((tiles, rows, deep), jnp.float32),
        scratch_shapes=[
            pltpu.VMEM((tiles, rows, deep), jnp.float32),
            pltpu.VMEM((rows, deep), jnp.float32),
            pltpu.VMEM((groups, rows, deep), jnp.float32),
            pltpu.VMEM((rows, deep), jnp.float32),
            dma((tiles,)),
            dma((tiles,)),
            dma((groups,)),
            dma((groups,)),
            dma((tiles,)),
            dma((tiles,)),
        ],
        compiler_params=pltpu.CompilerParams(
            collective_id=2, has_side_effects=True
        ),
    )(source)


def beam_coeffs(abs_speed):
    return (
        1.0 - 1.5 * abs_speed + 0.5 * abs_speed * abs_speed,
        2.0 * abs_speed - abs_speed * abs_speed,
        0.5 * abs_speed * abs_speed - 0.5 * abs_speed,
    )


def root_finder_guess(injection_contribution, collision_speed_factor, mode_pulsation):
    pseudo_kelvin_field = jnp.ones_like(injection_contribution)
    for newton_turn in range(NEWTON):
        dimensionless_pulsation = mode_pulsation[:, None] / pseudo_kelvin_field[None, :]
        heat_surplus = jnp.expm1(dimensionless_pulsation)
        mismatch_error = (
            jnp.sum(collision_speed_factor[:, None] / heat_surplus, axis=0) - injection_contribution
        )
        gradient_guess = (
            jnp.sum(
                collision_speed_factor[:, None]
                * dimensionless_pulsation
                * jnp.exp(dimensionless_pulsation)
                / (heat_surplus * heat_surplus),
                axis=0,
            )
            / pseudo_kelvin_field
        )
        pseudo_kelvin_field = jnp.clip(
            pseudo_kelvin_field - mismatch_error / gradient_guess,
            0.5 * pseudo_kelvin_field,
            2.0 * pseudo_kelvin_field,
        )
    return pseudo_kelvin_field


def on_device(
    phonon_heat_density,
    directions,
    quad_weight,
    mirror,
    band_courant,
    relax_rate,
    mode_heat_magnitude,
    mode_pulsation,
    wall_blocks,
    wall_count,
    wall_facet,
):
    local_dirs, bands, wide, high, deep = phonon_heat_density.shape
    tiles, groups = lax.axis_size("space"), lax.axis_size("dir")
    tile, group = lax.axis_index("space"), lax.axis_index("dir")
    rows = wide * high
    share = -(-bands // groups)
    extra = share * groups - bands
    dirs = directions.shape[1]
    orbits = dirs // OCT
    part = dirs // tiles
    part_orbits = orbits // tiles

    order, position = orbit_order(directions, mirror)
    own_facets = facet_grid(
        wall_blocks[0], wall_count[0], wall_facet[0], wide * high * deep // BLOCK
    ).astype(jnp.float32)
    def own_bands(values):
        return lax.dynamic_slice_in_dim(jnp.pad(values, (0, extra)), group * share, share)

    courant, rates = own_bands(band_courant), own_bands(relax_rate)
    magnitudes = own_bands(mode_heat_magnitude)
    pulsations = lax.dynamic_slice_in_dim(
        jnp.pad(mode_pulsation, (0, extra), constant_values=1.0), group * share, share
    )
    reps = lax.dynamic_slice_in_dim(
        order.reshape(orbits, OCT)[:, OCT - 1], tile * part_orbits, part_orbits
    )
    columns = []
    for axis_num in range(3):
        unit = jnp.abs(pick(directions[axis_num], reps))
        columns.extend(beam_coeffs(courant[:, None] * unit[None, :]))
    columns.append(rates[:, None] * pick(quad_weight, reps)[None, :])
    columns.append(jnp.broadcast_to(rates[:, None], columns[0].shape))
    coefs = jnp.stack(columns, axis=-1).reshape(share * part_orbits, len(columns))

    home = phonon_heat_density
    if extra:
        home = jnp.pad(home, ((0, 0), (0, extra), (0, 0), (0, 0), (0, 0)))
    field, source, facets = spread(
        tiles, groups, share, order, coefs, own_facets.reshape(rows, deep), home
    )
    collision_speed_factor = relax_rate * mode_heat_magnitude
    source = total(tiles, groups, source)
    kelvin = root_finder_guess(source.reshape(-1), collision_speed_factor, mode_pulsation)
    bose = magnitudes[:, None, None, None] / jnp.expm1(
        pulsations[:, None, None, None] / kelvin.reshape((1,) + source.shape)
    )
    moved, source = collect(tiles, groups, position, coefs, facets, field, bose, high)
    kelvin = root_finder_guess(source.reshape(-1), collision_speed_factor, mode_pulsation)
    kelvin = kelvin.reshape(wide, high, deep)
    moved = moved[:, :bands]
    home = mode_heat_magnitude[:, None, None, None] / jnp.expm1(
        mode_pulsation[:, None, None, None] / kelvin[None]
    )
    out = moved + relax_rate[None, :, None, None, None] * (home[None] - moved)
    return out, kelvin


def solution(mesh):
    in_specs = (
        P("dir", None, "space", None, None),
        P(),
        P(),
        P(),
        P(),
        P(),
        P(),
        P(),
        P("space", None),
        P("space"),
        P("space", None, None),
    )
    out_specs = (P("dir", None, "space", None, None), P("space", None, None))
    return jax.shard_map(
        on_device, mesh=mesh, in_specs=in_specs, out_specs=out_specs, check_vma=False
    )
```

```python
import functools

import jax
import jax.numpy as jnp
from jax import lax
from jax.experimental import pallas as pl
from jax.experimental.pallas import tpu as pltpu
from jax.sharding import PartitionSpec as P

NEWTON = 4
BLOCK = 128
OCT = 8


def pick(values, index):
    hits = index[:, None] == jnp.arange(values.shape[0], dtype=jnp.int32)[None, :]
    return jnp.sum(jnp.where(hits, values[None, :], jnp.zeros((), values.dtype)), axis=1)


def orbit_order(directions, mirror):
    count = directions.shape[1]
    ids = jnp.arange(count, dtype=jnp.int32)
    positive = (directions > 0).astype(jnp.int32)
    code = positive[0] + 2 * positive[1] + 4 * positive[2]
    rep = ids
    for axis_num in range(3):
        flipped = pick(mirror[axis_num], rep)
        rep = jnp.where(positive[axis_num] > 0, rep, flipped)
    is_rep = code == 7
    rank_of_rep = jnp.sum(
        jnp.where(is_rep[None, :] & (ids[None, :] < rep[:, None]), 1, 0), axis=1
    ).astype(jnp.int32)
    position = rank_of_rep * OCT + code
    order = jnp.sum(
        jnp.where(position[None, :] == ids[:, None], ids[None, :], 0), axis=1
    ).astype(jnp.int32)
    return order, position


def facet_grid(wall_blocks, wall_count, wall_facet, tile_blocks):
    slot_ids = jnp.arange(wall_blocks.shape[0], dtype=jnp.int32)
    hits = (wall_blocks[None, :] == jnp.arange(tile_blocks, dtype=jnp.int32)[:, None]) & (
        slot_ids < wall_count
    )[None, :]
    return jnp.sum(jnp.where(hits[:, :, None], wall_facet[None], 0), axis=1).astype(jnp.int32)


def roll(u, by, axis):
    return pltpu.roll(u, by % u.shape[axis], axis)


def unit_coeffs(scalars, band, orbit):
    order_ref, directions_ref, weight_ref, courant_ref, rate_ref = scalars
    bands = courant_ref.shape[0]
    real = band < bands
    index = jnp.minimum(band, bands - 1)
    courant, rate = courant_ref[index], jnp.where(real, rate_ref[index], 0.0)
    rep = order_ref[orbit * OCT + OCT - 1]
    coef = []
    for axis_num in range(3):
        coef.extend(beam_coeffs(courant * jnp.abs(directions_ref[axis_num, rep])))
    coef.append(rate * weight_ref[rep])
    return coef, rate


def surplus_of(q):
    series = jnp.ones_like(q)
    for n in range(9, 1, -1):
        series = 1.0 + series * (q * (1.0 / n))
    return jnp.where(q < 0.5, q * series, jnp.exp(q) - 1.0)


def newton(rate_ref, magnitude_ref, pulsation_ref, source):
    kelvin = jnp.ones_like(source)
    for newton_turn in range(NEWTON):
        inverse = 1.0 / kelvin

        def one(b, carry):
            mismatch, gradient = carry
            factor = rate_ref[b] * magnitude_ref[b]
            q = pulsation_ref[b] * inverse
            surplus = surplus_of(q)
            ratio = 1.0 / surplus
            term = factor * ratio
            return mismatch + term, gradient + term * q * ((surplus + 1.0) * ratio)

        zero = jnp.zeros_like(source)
        mismatch, gradient = lax.fori_loop(0, rate_ref.shape[0], one, (zero, zero), unroll=8)
        mismatch, gradient = mismatch - source, gradient * inverse
        kelvin = jnp.clip(kelvin - mismatch / gradient, 0.5 * kelvin, 2.0 * kelvin)
    return kelvin


def sweep_unit(high, tiles, coef, facets_ref, load, store):
    _, rows, width = facets_ref.shape
    row_id = lax.broadcasted_iota(jnp.int32, (rows, width), 0)
    height = row_id % high
    total = [jnp.zeros((rows, width), jnp.float32) for _ in range(tiles)]
    for o in range(OCT):
        way = [1 if o >> a & 1 else -1 for a in range(3)]
        cells = []
        for t in range(tiles):
            facets = facets_ref[t]
            u = load(t, o)
            for a in range(3):
                facing = float(2 * a + 1 if way[a] > 0 else 2 * a + 2)
                u = jnp.where(facets == facing, load(t, o ^ (1 << a)), u)
            cells.append(u)
        turned = [roll(u, high * way[0], 0) for u in cells]
        for t in range(tiles):
            up = (t - way[0]) % tiles
            edge = row_id < high if way[0] > 0 else row_id >= rows - high
            near = jnp.where(edge, turned[up], turned[t])
            u = coef[0] * cells[t] + coef[1] * near + coef[2] * cells[up]
            u = coef[3] * u + coef[4] * roll(u, way[1], 1) + coef[5] * roll(u, 2 * way[1], 1)
            wrap1 = height < 1 if way[2] > 0 else height >= high - 1
            wrap2 = height < 2 if way[2] > 0 else height >= high - 2
            near = jnp.where(wrap1, roll(u, (1 - high) * way[2], 0), roll(u, way[2], 0))
            far = jnp.where(wrap2, roll(u, (2 - high) * way[2], 0), roll(u, 2 * way[2], 0))
            u = coef[6] * u + coef[7] * near + coef[8] * far
            store(t, o, u)
            total[t] = total[t] + u
    return [coef[9] * total[t] for t in range(tiles)]


MESH = pl.DeviceIdType.MESH


def greet(tile, tiles, group, groups):
    barrier = pltpu.get_barrier_semaphore()
    for u in range(1, tiles):
        pl.semaphore_signal(
            barrier, inc=1, device_id=(lax.rem(tile + u, tiles), group), device_id_type=MESH
        )
    for t in range(1, groups):
        pl.semaphore_signal(
            barrier, inc=1, device_id=(tile, lax.rem(group + t, groups)), device_id_type=MESH
        )
    pl.semaphore_wait(barrier, tiles + groups - 2)


def remote(src, dst, send, recv, device):
    return pltpu.make_async_remote_copy(
        src_ref=src, dst_ref=dst, send_sem=send, recv_sem=recv, device_id=device, device_id_type=MESH
    )


CUTS = 2


def spread_kernel(
    tiles, groups, order_ref, directions_ref, weight_ref, courant_ref, rate_ref, magnitude_ref,
    pulsation_ref, facet_ref, home_ref, moved_ref, kelvin_ref, facets_ref, *scratch
):
    scalars = (order_ref, directions_ref, weight_ref, courant_ref, rate_ref)
    _, part, share, rows, deep = moved_ref.shape
    chunks = share * CUTS
    width = deep // CUTS
    landed, sorted_refs = scratch[:chunks], scratch[chunks : 2 * chunks]
    fields = scratch[2 * chunks : 2 * chunks + share]
    source_ref, near, summed, far, found = scratch[2 * chunks + share : 2 * chunks + share + 5]
    dir_send, dir_recv, tile_send, tile_recv, facet_send, facet_recv, own_sem = scratch[
        2 * chunks + share + 5 : 2 * chunks + share + 12
    ]
    near_send, near_recv, far_send, far_recv, last_send, last_recv = scratch[
        2 * chunks + share + 12 :
    ]
    local_dirs, _, wide, high, _ = home_ref.shape
    dirs, orbits = landed[0].shape[0], part // OCT
    tile, group = lax.axis_index("space"), lax.axis_index("dir")

    def lanes(c):
        return pl.ds(c % CUTS * width, width)

    own = [
        pltpu.make_async_copy(
            home_ref.at[:, group * share + c // CUTS, :, :, lanes(c)],
            landed[c].at[pl.ds(group * local_dirs, local_dirs)],
            own_sem.at[c],
        )
        for c in range(chunks)
    ]
    for copy in own:
        copy.start()
    own_facets = pltpu.make_async_copy(facet_ref, facets_ref.at[tile], own_sem.at[2 * chunks])
    own_facets.start()
    greet(tile, tiles, group, groups)

    third = []
    for u in range(1, tiles):
        copy = remote(
            facet_ref,
            facets_ref.at[tile],
            facet_send.at[u],
            facet_recv.at[u],
            (lax.rem(tile + u, tiles), group),
        )
        copy.start()
        third.append(copy)
    first = []
    for c in range(chunks):
        line = []
        for t in range(1, groups):
            peer = lax.rem(group + t, groups)
            copy = remote(
                home_ref.at[:, peer * share + c // CUTS, :, :, lanes(c)],
                landed[c].at[pl.ds(group * local_dirs, local_dirs)],
                dir_send.at[c, t],
                dir_recv.at[c, t],
                (tile, peer),
            )
            copy.start()
            line.append(copy)
        first.append(line)

    second = []
    source_ref[...] = jnp.zeros_like(source_ref)

    def sweep_band(k):
        for c in range(k * CUTS, (k + 1) * CUTS):
            second[c][0].wait()
            for copy in second[c][1:]:
                copy.wait_recv()

        def one(orbit, carry):
            def store(t, o, u):
                moved_ref[t, orbit * OCT + o, k] = u

            coef, _ = unit_coeffs(scalars, group * share + k, tile * orbits + orbit)
            sums = sweep_unit(
                high,
                tiles,
                coef,
                facets_ref,
                lambda t, o: fields[k][t, orbit * OCT + o],
                store,
            )
            for t in range(tiles):
                source_ref[t] = source_ref[t] + sums[t]
            return carry

        lax.fori_loop(0, orbits, one, 0)

    for c in range(chunks):
        own[c].wait()
        for copy in first[c]:
            copy.wait_recv()

        def move(j, carry):
            d = order_ref[j]
            for x in range(wide):
                sorted_refs[c][j, x * high : (x + 1) * high, :] = landed[c][d, x]
            return carry

        lax.fori_loop(0, dirs, move, 0, unroll=4)
        line = [
            pltpu.make_async_copy(
                sorted_refs[c].at[pl.ds(tile * part, part)],
                fields[c // CUTS].at[tile, :, :, lanes(c)],
                own_sem.at[chunks + c],
            )
        ]
        for u in range(1, tiles):
            peer = lax.rem(tile + u, tiles)
            line.append(
                remote(
                    sorted_refs[c].at[pl.ds(peer * part, part)],
                    fields[c // CUTS].at[tile, :, :, lanes(c)],
                    tile_send.at[c, u],
                    tile_recv.at[c, u],
                    (peer, group),
                )
            )
        for copy in line:
            copy.start()
        second.append(line)
        if c == 0:
            own_facets.wait()
            for copy in third:
                copy.wait_recv()
        if c >= CUTS and c % CUTS == 0:
            sweep_band(c // CUTS - 1)
    sweep_band(share - 1)

    copies = []
    for u in range(1, tiles):
        peer = lax.rem(tile + u, tiles)
        copy = remote(
            source_ref.at[peer], near.at[u], near_send.at[u], near_recv.at[u], (peer, group)
        )
        copy.start()
        copies.append(copy)
    value = source_ref[tile]
    for u in range(1, tiles):
        copies[u - 1].wait_recv()
        value = value + near[u]
    summed[...] = value
    gathers = []
    for t in range(1, groups):
        peer = lax.rem(group + t, groups)
        copy = remote(summed, far.at[group], far_send.at[t], far_recv.at[t], (tile, peer))
        copy.start()
        gathers.append(copy)
    far[group] = value
    for copy in gathers:
        copy.wait_recv()
    value = far[0]
    for g in range(1, groups):
        value = value + far[g]
    value = newton(rate_ref, magnitude_ref, pulsation_ref, value)
    found[...] = value
    lasts = []
    for u in range(1, tiles):
        peer = lax.rem(tile + u, tiles)
        copy = remote(found, kelvin_ref.at[tile], last_send.at[u], last_recv.at[u], (peer, group))
        copy.start()
        lasts.append(copy)
    kelvin_ref[tile] = value
    for copy in lasts:
        copy.wait_recv()
    for copy in copies + gathers + lasts:
        copy.wait_send()
    for line in first:
        for copy in line:
            copy.wait_send()
    for line in second:
        for copy in line[1:]:
            copy.wait_send()
    for copy in third:
        copy.wait_send()


def spread(tiles, groups, share, scalars, facets, home):
    local_dirs, _, wide, high, deep = home.shape
    dirs, rows = local_dirs * groups, wide * high
    part = dirs // tiles
    chunks, width = share * CUTS, deep // CUTS
    vmem = pl.BlockSpec(memory_space=pltpu.VMEM)
    smem = pl.BlockSpec(memory_space=pltpu.SMEM)
    dma = pltpu.SemaphoreType.DMA
    return pl.pallas_call(
        functools.partial(spread_kernel, tiles, groups),
        in_specs=[smem] * len(scalars) + [vmem, pl.BlockSpec(memory_space=pl.ANY)],
        out_specs=[vmem, vmem, vmem],
        out_shape=[
            jax.ShapeDtypeStruct((tiles, part, share, rows, deep), jnp.float32),
            jax.ShapeDtypeStruct((tiles, rows, deep), jnp.float32),
            jax.ShapeDtypeStruct((tiles, rows, deep), jnp.float32),
        ],
        scratch_shapes=[pltpu.VMEM((dirs, wide, high, width), jnp.float32)] * chunks
        + [pltpu.VMEM((dirs, rows, width), jnp.float32)] * chunks
        + [pltpu.VMEM((tiles, part, rows, deep), jnp.float32)] * share
        + [
            pltpu.VMEM((tiles, rows, deep), jnp.float32),
            pltpu.VMEM((tiles, rows, deep), jnp.float32),
            pltpu.VMEM((rows, deep), jnp.float32),
            pltpu.VMEM((groups, rows, deep), jnp.float32),
            pltpu.VMEM((rows, deep), jnp.float32),
            dma((chunks, groups)),
            dma((chunks, groups)),
            dma((chunks, tiles)),
            dma((chunks, tiles)),
            dma((tiles,)),
            dma((tiles,)),
            dma((2 * chunks + 1,)),
            dma((tiles,)),
            dma((tiles,)),
            dma((groups,)),
            dma((groups,)),
            dma((tiles,)),
            dma((tiles,)),
        ],
        compiler_params=pltpu.CompilerParams(collective_id=0, has_side_effects=True),
    )(*scalars, facets, home)


def collect_kernel(
    tiles, groups, position_ref, order_ref, directions_ref, weight_ref, courant_ref, rate_ref,
    magnitude_ref, pulsation_ref, facets_ref, field_ref, before_ref, home_ref, kelvin_ref, *scratch
):
    scalars = (order_ref, directions_ref, weight_ref, courant_ref, rate_ref)
    _, part, share, rows, deep = field_ref.shape
    chunks = share * CUTS
    width = deep // CUTS
    landed, sorted_refs = scratch[:chunks], scratch[chunks : 2 * chunks]
    swept = scratch[2 * chunks : 2 * chunks + share]
    now_ref, source_ref, near, summed, far, bose_ref = scratch[
        2 * chunks + share : 2 * chunks + share + 6
    ]
    dir_send, dir_recv, tile_send, tile_recv, near_send, near_recv, far_send, far_recv, own_sem = (
        scratch[2 * chunks + share + 6 :]
    )
    local_dirs, _, wide, high, _ = home_ref.shape
    dirs, orbits = part * tiles, part // OCT
    tile, group = lax.axis_index("space"), lax.axis_index("dir")
    greet(tile, tiles, group, groups)
    source_ref[...] = jnp.zeros_like(source_ref)
    first = []
    for k in range(share):
        band = jnp.minimum(group * share + k, courant_ref.shape[0] - 1)
        for t in range(tiles):
            bose_ref[t] = magnitude_ref[band] / surplus_of(pulsation_ref[band] / before_ref[t])

        def one(orbit, carry):
            coef, rate = unit_coeffs(scalars, group * share + k, tile * orbits + orbit)
            for t in range(tiles):
                bose = bose_ref[t]
                for o in range(OCT):
                    u = field_ref[t, orbit * OCT + o, k]
                    now_ref[t, o] = u + rate * (bose - u)

            def store(t, o, u):
                swept[k][t, orbit * OCT + o] = u

            sums = sweep_unit(
                high, tiles, coef, facets_ref, lambda t, o: now_ref[t, o], store
            )
            for t in range(tiles):
                source_ref[t] = source_ref[t] + sums[t]
            return carry

        lax.fori_loop(0, orbits, one, 0)
        for c in range(k * CUTS, (k + 1) * CUTS):
            lanes = pl.ds(c % CUTS * width, width)
            line = [
                pltpu.make_async_copy(
                    swept[k].at[tile, :, :, lanes],
                    landed[c].at[pl.ds(tile * part, part)],
                    own_sem.at[c],
                )
            ]
            for u in range(1, tiles):
                peer = lax.rem(tile + u, tiles)
                line.append(
                    remote(
                        swept[k].at[peer, :, :, lanes],
                        landed[c].at[pl.ds(tile * part, part)],
                        tile_send.at[c, u],
                        tile_recv.at[c, u],
                        (peer, group),
                    )
                )
            for copy in line:
                copy.start()
            first.append(line)
    nears = []
    for u in range(1, tiles):
        peer = lax.rem(tile + u, tiles)
        copy = remote(
            source_ref.at[peer], near.at[u], near_send.at[u], near_recv.at[u], (peer, group)
        )
        copy.start()
        nears.append(copy)
    second, fars = [], []
    for c in range(chunks):
        first[c][0].wait()
        for copy in first[c][1:]:
            copy.wait_recv()

        def move(d, carry):
            j = position_ref[d]
            for x in range(wide):
                sorted_refs[c][d, x] = landed[c][j, x * high : (x + 1) * high, :]
            return carry

        lax.fori_loop(0, dirs, move, 0, unroll=4)
        lanes = pl.ds(c % CUTS * width, width)
        line = [
            pltpu.make_async_copy(
                sorted_refs[c].at[pl.ds(group * local_dirs, local_dirs)],
                home_ref.at[:, group * share + c // CUTS, :, :, lanes],
                own_sem.at[chunks + c],
            )
        ]
        for t in range(1, groups):
            peer = lax.rem(group + t, groups)
            line.append(
                remote(
                    sorted_refs[c].at[pl.ds(peer * local_dirs, local_dirs)],
                    home_ref.at[:, group * share + c // CUTS, :, :, lanes],
                    dir_send.at[c, t],
                    dir_recv.at[c, t],
                    (tile, peer),
                )
            )
        for copy in line:
            copy.start()
        second.append(line)
        if c == chunks // 2 - 1:
            value = source_ref[tile]
            for u in range(1, tiles):
                nears[u - 1].wait_recv()
                value = value + near[u]
            summed[...] = value
            for t in range(1, groups):
                peer = lax.rem(group + t, groups)
                copy = remote(summed, far.at[group], far_send.at[t], far_recv.at[t], (tile, peer))
                copy.start()
                fars.append(copy)
            far[group] = value
    for copy in fars:
        copy.wait_recv()
    value = far[0]
    for g in range(1, groups):
        value = value + far[g]
    kelvin_ref[...] = newton(rate_ref, magnitude_ref, pulsation_ref, value)
    for line in second:
        line[0].wait()
        for copy in line[1:]:
            copy.wait_recv()
    for line in first + second:
        for copy in line[1:]:
            copy.wait_send()
    for copy in nears + fars:
        copy.wait_send()


def collect(tiles, groups, position, scalars, facets, field, kelvin, high):
    _, part, share, rows, deep = field.shape
    dirs = part * tiles
    local_dirs, wide = dirs // groups, rows // high
    chunks, width = share * CUTS, deep // CUTS
    vmem = pl.BlockSpec(memory_space=pltpu.VMEM)
    smem = pl.BlockSpec(memory_space=pltpu.SMEM)
    dma = pltpu.SemaphoreType.DMA
    return pl.pallas_call(
        functools.partial(collect_kernel, tiles, groups),
        in_specs=[smem] * (1 + len(scalars)) + [vmem, vmem, vmem],
        out_specs=[pl.BlockSpec(memory_space=pl.ANY), vmem],
        out_shape=[
            jax.ShapeDtypeStruct((local_dirs, share * groups, wide, high, deep), jnp.float32),
            jax.ShapeDtypeStruct((rows, deep), jnp.float32),
        ],
        scratch_shapes=[pltpu.VMEM((dirs, rows, width), jnp.float32)] * chunks
        + [pltpu.VMEM((dirs, wide, high, width), jnp.float32)] * chunks
        + [pltpu.VMEM((tiles, part, rows, deep), jnp.float32)] * share
        + [
            pltpu.VMEM((tiles, OCT, rows, deep), jnp.float32),
            pltpu.VMEM((tiles, rows, deep), jnp.float32),
            pltpu.VMEM((tiles, rows, deep), jnp.float32),
            pltpu.VMEM((rows, deep), jnp.float32),
            pltpu.VMEM((groups, rows, deep), jnp.float32),
            pltpu.VMEM((tiles, rows, deep), jnp.float32),
            dma((chunks, groups)),
            dma((chunks, groups)),
            dma((chunks, tiles)),
            dma((chunks, tiles)),
            dma((tiles,)),
            dma((tiles,)),
            dma((groups,)),
            dma((groups,)),
            dma((2 * chunks,)),
        ],
        compiler_params=pltpu.CompilerParams(collective_id=1, has_side_effects=True),
    )(position, *scalars, facets, field, kelvin)


def beam_coeffs(abs_speed):
    return (
        1.0 - 1.5 * abs_speed + 0.5 * abs_speed * abs_speed,
        2.0 * abs_speed - abs_speed * abs_speed,
        0.5 * abs_speed * abs_speed - 0.5 * abs_speed,
    )


def on_device(
    phonon_heat_density,
    directions,
    quad_weight,
    mirror,
    band_courant,
    relax_rate,
    mode_heat_magnitude,
    mode_pulsation,
    wall_blocks,
    wall_count,
    wall_facet,
):
    local_dirs, bands, wide, high, deep = phonon_heat_density.shape
    tiles, groups = lax.axis_size("space"), lax.axis_size("dir")
    rows = wide * high
    share = -(-bands // groups)
    extra = share * groups - bands

    order, position = orbit_order(directions, mirror)
    own_facets = facet_grid(
        wall_blocks[0], wall_count[0], wall_facet[0], wide * high * deep // BLOCK
    ).astype(jnp.float32)
    home = phonon_heat_density
    if extra:
        home = jnp.pad(home, ((0, 0), (0, extra), (0, 0), (0, 0), (0, 0)))
    scalars = (
        order,
        directions,
        quad_weight,
        band_courant,
        relax_rate,
        mode_heat_magnitude,
        mode_pulsation,
    )
    field, kelvin, facets = spread(
        tiles, groups, share, scalars, own_facets.reshape(rows, deep), home
    )
    moved, kelvin = collect(tiles, groups, position, scalars, facets, field, kelvin, high)
    kelvin = kelvin.reshape(wide, high, deep)
    moved = moved[:, :bands]
    home = mode_heat_magnitude[:, None, None, None] / jnp.expm1(
        mode_pulsation[:, None, None, None] / kelvin[None]
    )
    out = moved + relax_rate[None, :, None, None, None] * (home[None] - moved)
    return out, kelvin


def solution(mesh):
    in_specs = (
        P("dir", None, "space", None, None),
        P(),
        P(),
        P(),
        P(),
        P(),
        P(),
        P(),
        P("space", None),
        P("space"),
        P("space", None, None),
    )
    out_specs = (P("dir", None, "space", None, None), P("space", None, None))
    return jax.shard_map(
        on_device, mesh=mesh, in_specs=in_specs, out_specs=out_specs, check_vma=False
    )
```
